256 devices in a mesh: temporal: 8 (over z_lo, core), spatial: 16 (over y, x), head: 2 (over z_hi).
Axes of the slice: x: 4, y: 4, z: 8 (z_hi: 2, z_lo: 4; z = z_hi * 4 + z_lo), core: 2. Of those that a mesh axis runs over, the one named last changes fastest.
Arguments:
- queries: bfloat16 [32768, 2048], P(('temporal', 'spatial'), 'head'), may hold values from -120 to 120
- keys: bfloat16 [32768, 2048], P(('temporal', 'spatial'), 'head'), may hold values from -6 to 6
- values: bfloat16 [32768, 2048], P(('temporal', 'spatial'), 'head'), may hold values from -6 to 6
- window: int32 [8, 1, 16, 27], P('temporal', None, 'spatial'), may hold values from 0 to 1, as said below
Outputs:
- attended: bfloat16 [32768, 2048], P(('temporal', 'spatial'), 'head')
The draws below stay inside these ranges and needn't reach their ends.
Inputs may be any that keep to these rules, and one draw needn't show every extreme that they name: `window`: entry 9 (dt + 1) + 3 (dh + 1) + (dw + 1) of a tile's pattern admits the key tile at offset (dt, dh, dw) in tiles along frames, rows and columns; entry 13 is 1 for every tile.
All inputs are finite; a program needn't handle non-finite values.
Results may differ from the reference program's by a relative error of at most 0.0028.
Values may be sent and summed in bfloat16 or wider, within the bound.
No kernel may reach another device: no remote copies, remote signals or barrier semaphores. Data moves between devices by JAX's collectives and lax.ppermute only.
A program may use at most 64 MiB of HBM per device.

```python
import math
import jax
import jax.numpy as jnp
from jax import lax

D_HEAD = 128
HEADS = 16
TILE_T = 4
TILE_H = 8
TILE_W = 8
TH_TILES = 1
T_TILES = 8
W_TILES = 16
TOKENS = 32768
CHANNELS = 2048


def key_sample(key):
    folded = jax.random.fold_in(key, 7)
    first_key = jax.random.fold_in(folded, 0)
    extent = (TOKENS, HEADS * D_HEAD)
    sample = jax.random.normal(first_key, extent, jnp.float32)
    return jnp.clip(sample, -6.0, 6.0)


def draw_keys(key, part):
    return key_sample(key).astype(jnp.bfloat16)


def draw_queries(key, part):
    folded = jax.random.fold_in(key, 13)
    first_key = jax.random.fold_in(folded, 0)
    extent = (TOKENS, HEADS * D_HEAD)
    jitter = jax.random.normal(first_key, extent, jnp.float32)
    sample = 3.0 * jitter
    return jnp.clip(sample, -120.0, 120.0).astype(jnp.bfloat16)


def draw_window(key, part):
    folded = jax.random.fold_in(key, 3)
    levels = jax.random.randint(folded, (T_TILES, TH_TILES, W_TILES, 27), 0, 4)
    admitted = jnp.where(levels > 0, 1, 0).astype(jnp.int32)
    centre = jnp.arange(27, dtype=jnp.int32) == 13
    return jnp.where(centre[None, None, None, :], 1, admitted).astype(jnp.int32)


def block_scale(key, shape, cuts, smallest, largest):
    level = 1.0
    for position, blocks in cuts:
        heights = jax.random.uniform(jax.random.fold_in(jax.random.fold_in(key, 6), position), (blocks,), jnp.float32, smallest / len(cuts), largest / len(cuts))
        level = level * jnp.repeat(jnp.exp(heights), shape[position] // blocks).reshape((-1,) + (1,) * (len(shape) - 1 - position))
    return level


def scatter_about(own_key, shape, deviation, reach, shards=(), kind=jnp.bfloat16):
    values = deviation * jax.random.normal(own_key, shape, jnp.float32)
    if shards:
        values = values * block_scale(own_key, shape, shards, -0.22, 0.18)
    return jnp.clip(values, -reach, reach).astype(kind)


def setup_inputs(seed: int = 0) -> dict:
    seeds = jax.random.split(jax.random.key(seed), 5)
    queries = draw_queries(jax.random.fold_in(seeds[4], 71), 0)
    keys = draw_keys(jax.random.fold_in(seeds[4], 71), 0)
    values = scatter_about(seeds[2], (TOKENS, CHANNELS), 1.0, 6.0, ((0, 128), (1, 2)))
    window = draw_window(jax.random.fold_in(seeds[4], 71), 0)
    return dict(queries=queries, keys=keys, values=values, window=window)


def tile_mask(pattern, tile_row, first_row, window_rows, time_ok, width_ok):
    picked = []
    for offset in range(window_rows):
        height_step = first_row + offset - tile_row
        if -1 <= height_step <= 1:
            picked.append(pattern[:, height_step + 1, :] == 1)
        else:
            picked.append(jnp.zeros_like(pattern[:, 0, :]) == 1)
    chosen = jnp.stack(picked, axis=1)
    allowed = chosen & time_ok[:, None, None] & width_ok[None, None, :]
    return jnp.broadcast_to(allowed[:, None, :, None, :, None], (3, TILE_T, window_rows, TILE_H, 3, TILE_W)).reshape(-1)

def attend_all(query_tile, key_window, value_window, key_ok):
    scale = 1.0 / math.sqrt(D_HEAD)
    scores = jnp.einsum('qhd,khd->hqk', query_tile.astype(jnp.float32), key_window.astype(jnp.float32)) * scale
    scores = jnp.where(key_ok[None, None, :], scores, -jnp.inf)
    peak = lax.optimization_barrier(jnp.max(scores, axis=-1, keepdims=True))
    weights = jnp.exp(scores - peak)
    total = lax.optimization_barrier(jnp.sum(weights, axis=-1))
    rounded = lax.optimization_barrier(weights.astype(jnp.bfloat16))
    mixed = jnp.einsum('hqk,khd->qhd', rounded.astype(jnp.float32), value_window.astype(jnp.float32))
    mixed = mixed / jnp.transpose(total)[:, :, None]
    return mixed.astype(jnp.bfloat16).reshape(mixed.shape[0], -1)

def reference(queries, keys, values, window):
    channels = HEADS * D_HEAD
    tile_size = TILE_T * TILE_H * TILE_W
    shape_tiles = (T_TILES, TILE_T, TH_TILES, TILE_H, W_TILES, TILE_W, channels)
    query_tiles = queries.reshape(shape_tiles)
    padding = ((1, 1), (0, 0), (0, 0), (0, 0), (1, 1), (0, 0), (0, 0))
    key_padded = jnp.pad(keys.reshape(shape_tiles), padding)
    value_padded = jnp.pad(values.reshape(shape_tiles), padding)
    window_rows = min(3, TH_TILES)
    offsets = jnp.arange(3, dtype=jnp.int32) - 1
    results = []
    for tile_row in range(TH_TILES):
        first_row = min(max(tile_row - 1, 0), TH_TILES - window_rows)

        def one_tile(flat_index):
            time_tile = flat_index // W_TILES
            width_tile = flat_index % W_TILES
            zero = jnp.zeros((), jnp.int32)
            query_tile = lax.dynamic_slice(query_tiles, (time_tile, zero, zero + tile_row, zero, width_tile, zero, zero), (1, TILE_T, 1, TILE_H, 1, TILE_W, channels)).reshape(tile_size, HEADS, D_HEAD)
            corner = (time_tile, zero, zero + first_row, zero, width_tile, zero, zero)
            extent = (3, TILE_T, window_rows, TILE_H, 3, TILE_W, channels)
            key_window = lax.dynamic_slice(key_padded, corner, extent).reshape(-1, HEADS, D_HEAD)
            value_window = lax.dynamic_slice(value_padded, corner, extent).reshape(-1, HEADS, D_HEAD)
            pattern = lax.dynamic_slice(window, (time_tile, zero + tile_row, width_tile, zero), (1, 1, 1, 27)).reshape(3, 3, 3)
            time_index = time_tile + offsets
            width_index = width_tile + offsets
            time_ok = (time_index >= 0) & (time_index < T_TILES)
            width_ok = (width_index >= 0) & (width_index < W_TILES)
            key_ok = tile_mask(pattern, tile_row, first_row, window_rows, time_ok, width_ok)
            return attend_all(query_tile, key_window, value_window, key_ok)
        flat = lax.map(one_tile, jnp.arange(T_TILES * W_TILES, dtype=jnp.int32))
        results.append(flat.reshape(T_TILES, W_TILES, TILE_T, TILE_H, TILE_W, channels))
    stacked = jnp.stack(results, axis=2)
    ordered = jnp.transpose(stacked, (0, 3, 2, 4, 1, 5, 6))
    return ordered.reshape(TOKENS, channels)
```

```python
import math

import jax
import jax.numpy as jnp
from jax import lax
from jax.experimental import pallas as pl
from jax.experimental.pallas import tpu as pltpu
from jax.sharding import PartitionSpec as P

D = 128
HEADS = 8
TILES = 8
COLS = 16
HALO = 9
BIG = 3.0e38
SCALE = math.log2(math.e) / math.sqrt(D)


def pack_kernel(q_ref, k_ref, v_ref, w_ref, kv_out, q_out):
    pattern = w_ref[...].astype(jnp.float32)
    rows = lax.broadcasted_iota(jnp.int32, (16, 128), 0)
    lanes = lax.broadcasted_iota(jnp.int32, (16, 128), 1)
    pick = 9 * (rows // 3) + 3 + rows % 3
    kept = jnp.where(lanes == pick, jnp.broadcast_to(pattern, (16, 128)), 0.0)
    marks = jnp.broadcast_to(jnp.sum(kept, axis=1, keepdims=True), (16, 128))
    low = marks[0:8].astype(jnp.bfloat16)
    high = marks[8:16].astype(jnp.bfloat16)
    for h in range(HEADS):
        lane = pl.ds(h * D, D)
        for half in range(2):
            d = 2 * h + half
            for r in range(2):
                kv_out[d, 0:HALO, r] = k_ref[r, pl.ds(7 * half, HALO), :, lane]
                kv_out[d, HALO : 2 * HALO, r] = v_ref[r, pl.ds(7 * half, HALO), :, lane]
                q_out[d, 0:TILES, r] = q_ref[r, pl.ds(8 * half, TILES), :, lane]
            q_out[d, TILES, 0] = low
            q_out[d, TILES, 1] = high


def pack(q, k, v, window):
    shaped = [x.reshape(2, COLS, 8, HEADS * D) for x in (q, k, v)]
    pattern = jnp.pad(window.reshape(1, 27), ((0, 0), (0, 101)))
    vmem = pl.BlockSpec(memory_space=pltpu.VMEM)
    return pl.pallas_call(
        pack_kernel,
        out_shape=(
            jax.ShapeDtypeStruct((16, 2 * HALO, 2, 8, D), jnp.bfloat16),
            jax.ShapeDtypeStruct((16, TILES + 1, 2, 8, D), jnp.bfloat16),
        ),
        in_specs=[vmem] * 4,
        out_specs=(vmem, vmem),
        name="pack",
    )(*shaped, pattern)


def attend_kernel(q_ref, prev_ref, own_ref, next_ref, o_ref, s_ref):
    t = lax.axis_index("temporal")
    half = lax.axis_index("spatial") % 2

    def tile(w, carry):
        q = q_ref[:, w].reshape(256, D)
        marks = q_ref[half * TILES + w, TILES].astype(jnp.float32)
        column = half * TILES + w
        tops, oks = [], []
        for a, ref in enumerate((prev_ref, own_ref, next_ref)):
            t_ok = (t + a - 1 >= 0) & (t + a - 1 < 8)
            for b in range(3):
                w_ok = (column + b - 1 >= 0) & (column + b - 1 < COLS)
                index = jnp.clip(w + b - 1 + half, 0, HALO - 1)
                j = 3 * a + b
                k = ref[:, index].reshape(256, D)
                s = lax.dot_general(
                    q, k, (((1,), (1,)), ((), ())), preferred_element_type=jnp.float32
                )
                s_ref[:, j * 256 : (j + 1) * 256] = s
                gate = jnp.where(t_ok & w_ok, 1.0, 0.0)
                ok = jnp.broadcast_to(marks[j : j + 1, 0:1] * gate, (256, 1)) > 0.5
                tops.append(jnp.where(ok, jnp.max(s, axis=1, keepdims=True), -BIG))
                oks.append(ok)
        peak = tops[0]
        for x in tops[1:]:
            peak = jnp.maximum(peak, x)
        peak = peak * SCALE
        total = jnp.zeros((256, 128), jnp.float32)
        acc = jnp.zeros((256, D), jnp.float32)
        for a, ref in enumerate((prev_ref, own_ref, next_ref)):
            for b in range(3):
                index = jnp.clip(w + b - 1 + half, 0, HALO - 1) + HALO
                j = 3 * a + b
                v = ref[:, index].reshape(256, D)
                shift = jnp.where(oks[j], peak, BIG)
                p = jnp.exp2(s_ref[:, j * 256 : (j + 1) * 256] * SCALE - shift)
                total = total + p[:, 0:128] + p[:, 128:256]
                acc = acc + jnp.dot(
                    p.astype(jnp.bfloat16), v, preferred_element_type=jnp.float32
                )
        out = acc / jnp.sum(total, axis=1, keepdims=True)
        o_ref[:, w] = out.astype(jnp.bfloat16).reshape(16, 16, D)
        return carry

    lax.fori_loop(0, TILES, tile, 0)


def attend(q, prev, own, nxt):
    vmem = pl.BlockSpec(memory_space=pltpu.VMEM)
    return pl.pallas_call(
        attend_kernel,
        out_shape=jax.ShapeDtypeStruct((16, TILES, 16, D), jnp.bfloat16),
        in_specs=[vmem] * 4,
        out_specs=vmem,
        scratch_shapes=[pltpu.VMEM((256, 9 * 256), jnp.float32)],
        name="attend",
    )(q, prev, own, nxt)


def unpack_kernel(x_ref, o_ref):
    for h in range(HEADS):
        for half in range(2):
            for r in range(2):
                o_ref[r, pl.ds(8 * half, TILES), :, pl.ds(h * D, D)] = x_ref[2 * h + half, :, r]


def unpack(x):
    vmem = pl.BlockSpec(memory_space=pltpu.VMEM)
    out = pl.pallas_call(
        unpack_kernel,
        out_shape=jax.ShapeDtypeStruct((2, COLS, 8, HEADS * D), jnp.bfloat16),
        in_specs=[vmem],
        out_specs=vmem,
        name="unpack",
    )(x)
    return out.reshape(256, HEADS * D)


def swap(x):
    return lax.all_to_all(x, "spatial", split_axis=0, concat_axis=0, tiled=True)


def body(queries, keys, values, window):
    kv_send, q_send = pack(queries, keys, values, window)
    own = swap(kv_send.reshape(16, 2 * HALO, 16, D))
    steps = lax.axis_size("temporal")
    up = [(i, i + 1) for i in range(steps - 1)]
    down = [(j, i) for i, j in up]
    prev = lax.ppermute(own, "temporal", up)
    nxt = lax.ppermute(own, "temporal", down)
    q = swap(q_send.reshape(16, TILES + 1, 16, D))
    out = attend(q, prev, own, nxt)
    back = swap(out)
    return unpack(back.reshape(16, TILES, 2, 8, D))


def solution(mesh):
    return jax.shard_map(
        body,
        mesh=mesh,
        in_specs=(
            P(("temporal", "spatial"), "head"),
            P(("temporal", "spatial"), "head"),
            P(("temporal", "spatial"), "head"),
            P("temporal", None, "spatial", None),
        ),
        out_specs=P(("temporal", "spatial"), "head"),
        check_vma=False,
    )
```

```python
import math

import jax
import jax.numpy as jnp
from jax import lax
from jax.experimental import pallas as pl
from jax.experimental.pallas import tpu as pltpu
from jax.sharding import PartitionSpec as P

D = 128
HEADS = 8
TILES = 8
COLS = 16
HALO = 9
BIG = 3.0e38
SCALE = math.log2(math.e) / math.sqrt(D)


def resident(x):
    return pltpu.with_memory_space_constraint(x, pltpu.VMEM)


def pack_kernel(q_ref, k_ref, v_ref, w_ref, kv_out, q_out):
    pattern = w_ref[...].astype(jnp.float32)
    pattern = jnp.concatenate([pattern, jnp.zeros((1, 101), jnp.float32)], axis=1)
    rows = lax.broadcasted_iota(jnp.int32, (16, 128), 0)
    lanes = lax.broadcasted_iota(jnp.int32, (16, 128), 1)
    pick = 9 * (rows // 3) + 3 + rows % 3
    kept = jnp.where(lanes == pick, jnp.broadcast_to(pattern, (16, 128)), 0.0)
    marks = jnp.broadcast_to(jnp.sum(kept, axis=1, keepdims=True), (16, 128))
    low = marks[0:8].astype(jnp.bfloat16)
    high = marks[8:16].astype(jnp.bfloat16)
    for h in range(HEADS):
        lane = pl.ds(h * D, D)
        for half in range(2):
            d = 2 * h + half
            for r in range(2):
                kv_out[d, 0:HALO, r] = k_ref[r, pl.ds(7 * half, HALO), :, lane]
                kv_out[d, HALO : 2 * HALO, r] = v_ref[r, pl.ds(7 * half, HALO), :, lane]
                q_out[d, 0:TILES, r] = q_ref[r, pl.ds(8 * half, TILES), :, lane]
            q_out[d, TILES, 0] = low
            q_out[d, TILES, 1] = high


def pack(q, k, v, window):
    shaped = [x.reshape(2, COLS, 8, HEADS * D) for x in (q, k, v)]
    pattern = window.reshape(1, 27)
    vmem = pl.BlockSpec(memory_space=pltpu.VMEM)
    return pl.pallas_call(
        pack_kernel,
        out_shape=(
            pltpu.VMEM((16, 2 * HALO, 2, 8, D), jnp.bfloat16),
            pltpu.VMEM((16, TILES + 1, 2, 8, D), jnp.bfloat16),
        ),
        in_specs=[vmem] * 4,
        out_specs=(vmem, vmem),
        name="pack",
        compiler_params=pltpu.CompilerParams(vmem_limit_bytes=16 << 20),
    )(*shaped, pattern)


def attend_kernel(q_ref, prev_ref, own_ref, next_ref, o_ref, s_ref):
    t = lax.axis_index("temporal")
    half = lax.axis_index("spatial") % 2

    def tile(w, carry):
        q = q_ref[:, w].reshape(256, D)
        marks = q_ref[half * TILES + w, TILES].astype(jnp.float32)
        column = half * TILES + w
        tops, oks = [], []
        for a, ref in enumerate((prev_ref, own_ref, next_ref)):
            t_ok = (t + a - 1 >= 0) & (t + a - 1 < 8)
            for b in range(3):
                w_ok = (column + b - 1 >= 0) & (column + b - 1 < COLS)
                index = jnp.clip(w + b - 1 + half, 0, HALO - 1)
                j = 3 * a + b
                k = ref[:, index].reshape(256, D)
                s = lax.dot_general(
                    q, k, (((1,), (1,)), ((), ())), preferred_element_type=jnp.float32
                )
                s_ref[:, j * 256 : (j + 1) * 256] = s
                gate = jnp.where(t_ok & w_ok, 1.0, 0.0)
                ok = jnp.broadcast_to(marks[j : j + 1, 0:1] * gate, (256, 1)) > 0.5
                tops.append(jnp.where(ok, jnp.max(s, axis=1, keepdims=True), -BIG))
                oks.append(ok)
        peak = tops[0]
        for x in tops[1:]:
            peak = jnp.maximum(peak, x)
        peak = peak * SCALE
        total = jnp.zeros((256, 128), jnp.float32)
        acc = jnp.zeros((256, D), jnp.float32)
        for a, ref in enumerate((prev_ref, own_ref, next_ref)):
            for b in range(3):
                index = jnp.clip(w + b - 1 + half, 0, HALO - 1) + HALO
                j = 3 * a + b
                v = ref[:, index].reshape(256, D)
                shift = jnp.where(oks[j], peak, BIG)
                p = jnp.exp2(s_ref[:, j * 256 : (j + 1) * 256] * SCALE - shift)
                total = total + p[:, 0:128] + p[:, 128:256]
                acc = acc + jnp.dot(
                    p.astype(jnp.bfloat16), v, preferred_element_type=jnp.float32
                )
        out = acc / jnp.sum(total, axis=1, keepdims=True)
        o_ref[:, w] = out.astype(jnp.bfloat16).reshape(16, 16, D)
        return carry

    lax.fori_loop(0, TILES, tile, 0)


def attend(q, prev, own, nxt):
    vmem = pl.BlockSpec(memory_space=pltpu.VMEM)
    return pl.pallas_call(
        attend_kernel,
        out_shape=pltpu.VMEM((16, TILES, 16, D), jnp.bfloat16),
        in_specs=[vmem] * 4,
        out_specs=vmem,
        scratch_shapes=[pltpu.VMEM((256, 9 * 256), jnp.float32)],
        name="attend",
        compiler_params=pltpu.CompilerParams(vmem_limit_bytes=24 << 20),
    )(*[resident(x) for x in (q, prev, own, nxt)])


def unpack_kernel(x_ref, o_ref):
    for h in range(HEADS):
        for half in range(2):
            for r in range(2):
                o_ref[r, pl.ds(8 * half, TILES), :, pl.ds(h * D, D)] = x_ref[2 * h + half, :, r]


def unpack(x):
    vmem = pl.BlockSpec(memory_space=pltpu.VMEM)
    out = pl.pallas_call(
        unpack_kernel,
        out_shape=jax.ShapeDtypeStruct((2, COLS, 8, HEADS * D), jnp.bfloat16),
        in_specs=[vmem],
        out_specs=vmem,
        name="unpack",
        compiler_params=pltpu.CompilerParams(vmem_limit_bytes=8 << 20),
    )(resident(x))
    return out.reshape(256, HEADS * D)


def swap(x):
    return lax.all_to_all(x, "spatial", split_axis=0, concat_axis=0, tiled=True)


def body(queries, keys, values, window):
    kv_send, q_send = pack(queries, keys, values, window)
    own = swap(kv_send.reshape(16, 2 * HALO, 16, D))
    steps = lax.axis_size("temporal")
    up = [(i, i + 1) for i in range(steps - 1)]
    down = [(j, i) for i, j in up]
    prev = lax.ppermute(own, "temporal", up)
    nxt = lax.ppermute(own, "temporal", down)
    q = swap(q_send.reshape(16, TILES + 1, 16, D))
    out = attend(q, prev, own, nxt)
    back = swap(out)
    return unpack(back.reshape(16, TILES, 2, 8, D))


def solution(mesh):
    return jax.shard_map(
        body,
        mesh=mesh,
        in_specs=(
            P(("temporal", "spatial"), "head"),
            P(("temporal", "spatial"), "head"),
            P(("temporal", "spatial"), "head"),
            P("temporal", None, "spatial", None),
        ),
        out_specs=P(("temporal", "spatial"), "head"),
        check_vma=False,
    )
```

```python
import math

import jax
import jax.numpy as jnp
from jax import lax
from jax.experimental import pallas as pl
from jax.experimental.pallas import tpu as pltpu
from jax.sharding import PartitionSpec as P

D = 128
HEADS = 8
TILES = 8
COLS = 16
HALO = 9
KV_ROWS = 2 * HALO * 16
Q_ROW = KV_ROWS
MARK_ROW = KV_ROWS + TILES * 16
ROWS = MARK_ROW + 8
BIG = 3.0e38
SCALE = math.log2(math.e) / math.sqrt(D)
VMEM = pl.BlockSpec(memory_space=pltpu.VMEM)


def resident(x):
    return pltpu.with_memory_space_constraint(x, pltpu.VMEM)


def limit(mib):
    return pltpu.CompilerParams(vmem_limit_bytes=mib << 20)


def pack_kernel(q_hbm, k_hbm, v_hbm, w_ref, out, buf, sems):
    copies = []
    for i, src in enumerate((k_hbm, v_hbm, q_hbm)):
        for r in range(2):
            for part in range(2):
                cut = pl.ds(8 * part, 8)
                copies.append(
                    pltpu.make_async_copy(
                        src.at[r, cut], buf.at[i, r, cut], sems.at[i, r, part]
                    )
                )
    for copy in copies:
        copy.start()
    pattern = w_ref[...].astype(jnp.float32)
    pattern = jnp.concatenate([pattern, jnp.zeros((1, 101), jnp.float32)], axis=1)
    row = lax.broadcasted_iota(jnp.int32, (8, 128), 0)
    lanes = lax.broadcasted_iota(jnp.int32, (8, 128), 1)
    entry = row + jnp.where(row >= 4, 1, 0)
    pick = 9 * (entry // 3) + 3 + entry % 3
    kept = jnp.where(lanes == pick, jnp.broadcast_to(pattern, (8, 128)), 0.0)
    marks = jnp.broadcast_to(jnp.sum(kept, axis=1, keepdims=True), (8, 128))
    marks = marks.astype(jnp.bfloat16)
    for d in range(16):
        out[d, MARK_ROW // 8] = marks
    for i in range(3):
        for copy in copies[4 * i : 4 * i + 4]:
            copy.wait()
        count, step = (TILES, 8) if i == 2 else (HALO, 7)
        base = (0, 2 * HALO, Q_ROW // 8)[i]
        for h in range(HEADS):
            for half in range(2):
                for r in range(2):
                    for w in range(count):
                        out[2 * h + half, base + 2 * w + r] = buf[
                            i, r, step * half + w, :, pl.ds(h * D, D)
                        ]


def pack(q, k, v, window):
    shaped = [
        pltpu.with_memory_space_constraint(x.reshape(2, COLS, 8, HEADS * D), pltpu.HBM)
        for x in (q, k, v)
    ]
    anywhere = pl.BlockSpec(memory_space=pl.ANY)
    return pl.pallas_call(
        pack_kernel,
        out_shape=pltpu.VMEM((16, ROWS // 8, 8, D), jnp.bfloat16),
        in_specs=[anywhere] * 3 + [VMEM],
        out_specs=VMEM,
        scratch_shapes=[
            pltpu.VMEM((3, 2, COLS, 8, HEADS * D), jnp.bfloat16),
            pltpu.SemaphoreType.DMA((3, 2, 2)),
        ],
        compiler_params=limit(16),
        name="pack",
    )(*shaped, window.reshape(1, 27))


def cut_kernel(all_ref, kv_ref):
    kv_ref[...] = all_ref[:, 0:KV_ROWS]


def cut(everything):
    return pl.pallas_call(
        cut_kernel,
        out_shape=pltpu.VMEM((16, KV_ROWS, D), jnp.bfloat16),
        in_specs=[VMEM],
        out_specs=VMEM,
        compiler_params=limit(8),
        name="cut",
    )(resident(everything))


def take(ref, row):
    start = pl.multiple_of(row, 16)
    return ref[:, pl.ds(start, 16), :].reshape(256, D)


def shard_place():
    t = lax.axis_index("temporal")
    half = lax.axis_index("spatial") % 2
    return t, half


def key_index(w, b, half):
    return jnp.clip(w + b - 1 + half, 0, HALO - 1)


def columns_ok(column, b):
    return (column + b - 1 >= 0) & (column + b - 1 < COLS)


def scores(q, k):
    return lax.dot_general(q, k, (((1,), (1,)), ((), ())), preferred_element_type=jnp.float32)


def weigh(s_ref, slot, refs, oks, shift_from, w, half, total, acc):
    for n, (ref, b) in enumerate(refs):
        v = take(ref, (key_index(w, b, half) + HALO) * 16)
        shift = shift_from if oks[n] is None else jnp.where(oks[n], shift_from, BIG)
        p = jnp.exp2(s_ref[slot, :, n * 256 : (n + 1) * 256] * SCALE - shift)
        part = p[:, 0:128] + p[:, 128:256]
        total = part if total is None else total + part
        mixed = jnp.dot(p.astype(jnp.bfloat16), v, preferred_element_type=jnp.float32)
        acc = mixed if acc is None else acc + mixed
    return total, acc


def near_kernel(all_ref, mate_ref, acc_ref, peak_ref, total_ref, s_ref):
    t, half = shard_place()
    even = t % 2 == 0

    def tile(w, slot):
        column = half * TILES + w
        q = take(all_ref, Q_ROW + 16 * w)
        marks = all_ref[column, pl.ds(MARK_ROW, 8), :].astype(jnp.float32)
        refs, oks, top = [], [], None
        for ref in (all_ref, mate_ref):
            for b in range(3):
                n = len(refs)
                k = take(ref, key_index(w, b, half) * 16)
                s = scores(q, k)
                s_ref[slot, :, n * 256 : (n + 1) * 256] = s
                high = jnp.max(s, axis=1, keepdims=True)
                if ref is all_ref:
                    mark = None if b == 1 else marks[3 + b // 2 : 4 + b // 2, 0:1]
                else:
                    mark = jnp.where(even, marks[5 + b : 6 + b, 0:1], marks[b : b + 1, 0:1])
                if mark is None:
                    ok = None
                else:
                    gate = 1.0 if b == 1 else jnp.where(columns_ok(column, b), 1.0, 0.0)
                    ok = jnp.broadcast_to(mark * gate, (256, 1)) > 0.5
                    high = jnp.where(ok, high, -BIG)
                top = high if top is None else jnp.maximum(top, high)
                refs.append((ref, b))
                oks.append(ok)
        peak = top * SCALE
        total, acc = weigh(s_ref, slot, refs, oks, peak, w, half, None, None)
        acc_ref[w] = acc
        total_ref[w] = total
        peak_ref[w] = jnp.broadcast_to(peak, (256, 128))

    def pair(i, carry):
        tile(2 * i, 0)
        tile(2 * i + 1, 1)
        return carry

    lax.fori_loop(0, TILES // 2, pair, 0)


def near(everything, mate):
    part = pltpu.VMEM((TILES, 256, D), jnp.float32)
    return pl.pallas_call(
        near_kernel,
        out_shape=(part, part, part),
        in_specs=[VMEM] * 2,
        out_specs=(VMEM,) * 3,
        scratch_shapes=[pltpu.VMEM((2, 256, 6 * 256), jnp.float32)],
        compiler_params=limit(16),
        cost_estimate=pl.CostEstimate(
            flops=8 * 6 * 4 * 256 * 256 * D, bytes_accessed=6 << 20, transcendentals=8 * 6 * 65536
        ),
        name="near",
    )(resident(everything), resident(mate))


def far_kernel(all_ref, far_ref, acc_ref, peak_ref, total_ref, o_ref, s_ref):
    t, half = shard_place()
    even = t % 2 == 0
    t_ok = jnp.where(even, t > 0, t < 7)

    def tile(w, slot):
        column = half * TILES + w
        q = take(all_ref, Q_ROW + 16 * w)
        marks = all_ref[column, pl.ds(MARK_ROW, 8), :].astype(jnp.float32)
        refs, oks = [], []
        before = peak_ref[w, :, 0:1]
        top = None
        for b in range(3):
            k = take(far_ref, key_index(w, b, half) * 16)
            s = scores(q, k)
            s_ref[slot, :, b * 256 : (b + 1) * 256] = s
            mark = jnp.where(even, marks[b : b + 1, 0:1], marks[5 + b : 6 + b, 0:1])
            gate = jnp.where(columns_ok(column, b) & t_ok, 1.0, 0.0)
            ok = jnp.broadcast_to(mark * gate, (256, 1)) > 0.5
            high = jnp.where(ok, jnp.max(s, axis=1, keepdims=True), -BIG)
            top = high if top is None else jnp.maximum(top, high)
            refs.append((far_ref, b))
            oks.append(ok)
        peak = jnp.maximum(before, jnp.where(top > -BIG, top, -BIG / 4) * SCALE)
        fade = jnp.exp2(before - peak)
        total, acc = weigh(
            s_ref, slot, refs, oks, peak, w, half, total_ref[w] * fade, acc_ref[w] * fade
        )
        out = acc / jnp.sum(total, axis=1, keepdims=True)
        o_ref[:, pl.ds(pl.multiple_of(16 * w, 16), 16), :] = out.astype(jnp.bfloat16).reshape(
            16, 16, D
        )

    def pair(i, carry):
        tile(2 * i, 0)
        tile(2 * i + 1, 1)
        return carry

    lax.fori_loop(0, TILES // 2, pair, 0)


def far(everything, other, parts):
    return pl.pallas_call(
        far_kernel,
        out_shape=pltpu.VMEM((16, TILES * 16, D), jnp.bfloat16),
        in_specs=[VMEM] * 5,
        out_specs=VMEM,
        scratch_shapes=[pltpu.VMEM((2, 256, 3 * 256), jnp.float32)],
        compiler_params=limit(16),
        name="far",
    )(*[resident(x) for x in (everything, other, *parts)])


def unpack_kernel(x_ref, o_ref):
    for h in range(HEADS):
        for half in range(2):
            for r in range(2):
                o_ref[r, pl.ds(8 * half, TILES), :, pl.ds(h * D, D)] = x_ref[2 * h + half, :, r]


def unpack(x):
    out = pl.pallas_call(
        unpack_kernel,
        out_shape=jax.ShapeDtypeStruct((2, COLS, 8, HEADS * D), jnp.bfloat16),
        in_specs=[VMEM],
        out_specs=VMEM,
        compiler_params=limit(8),
        name="unpack",
    )(resident(x))
    return out.reshape(256, HEADS * D)


def swap(x):
    return lax.all_to_all(x, "spatial", split_axis=0, concat_axis=0, tiled=True)


def body(queries, keys, values, window):
    everything = swap(pack(queries, keys, values, window).reshape(16, ROWS, D))
    kv = cut(everything)
    steps = lax.axis_size("temporal")
    across = [(i, i + 1) for i in range(1, steps - 1, 2)]
    mates = [(i, i + 1) for i in range(0, steps, 2)]
    other = lax.ppermute(kv, "temporal", across + [(j, i) for i, j in across])
    mate = lax.ppermute(kv, "temporal", mates + [(j, i) for i, j in mates])
    parts = near(everything, mate)
    out = far(everything, other, parts)
    back = swap(out)
    return unpack(back.reshape(16, TILES, 2, 8, D))


def solution(mesh):
    return jax.shard_map(
        body,
        mesh=mesh,
        in_specs=(
            P(("temporal", "spatial"), "head"),
            P(("temporal", "spatial"), "head"),
            P(("temporal", "spatial"), "head"),
            P("temporal", None, "spatial", None),
        ),
        out_specs=P(("temporal", "spatial"), "head"),
        check_vma=False,
    )
```

```python
import functools
import math

import jax
import jax.numpy as jnp
from jax import lax
from jax.experimental import pallas as pl
from jax.experimental.pallas import tpu as pltpu
from jax.sharding import PartitionSpec as P

D = 128
HEADS = 8
TILES = 8
COLS = 16
HALO = 9
KV_ROWS = 2 * HALO * 16
Q_ROW = KV_ROWS
MARK_ROW = KV_ROWS + TILES * 16
ROWS = MARK_ROW + 8
FIRST = 7 * 16
LAST = 2 * 16
EARLY = 5
BIG = 3.0e38
SCALE = math.log2(math.e) / math.sqrt(D)
VMEM = pl.BlockSpec(memory_space=pltpu.VMEM)


def resident(x):
    return pltpu.with_memory_space_constraint(x, pltpu.VMEM)


def limit(mib):
    return pltpu.CompilerParams(vmem_limit_bytes=mib << 20)


def pack_kernel(q_hbm, k_hbm, v_hbm, w_hbm, out, buf, w_ref, sems, w_sem):
    fetch = pltpu.make_async_copy(w_hbm, w_ref, w_sem)
    fetch.start()
    copies = []
    for i, src in enumerate((k_hbm, v_hbm, q_hbm)):
        for r in range(2):
            for part in range(2):
                cut = pl.ds(8 * part, 8)
                copies.append(
                    pltpu.make_async_copy(
                        src.at[r, cut], buf.at[i, r, cut], sems.at[i, r, part]
                    )
                )
    for copy in copies:
        copy.start()
    fetch.wait()
    pattern = w_ref[...].astype(jnp.float32)
    pattern = jnp.concatenate([pattern, jnp.zeros((1, 101), jnp.float32)], axis=1)
    row = lax.broadcasted_iota(jnp.int32, (8, 128), 0)
    lanes = lax.broadcasted_iota(jnp.int32, (8, 128), 1)
    entry = row + jnp.where(row >= 4, 1, 0)
    pick = 9 * (entry // 3) + 3 + entry % 3
    kept = jnp.where(lanes == pick, jnp.broadcast_to(pattern, (8, 128)), 0.0)
    marks = jnp.broadcast_to(jnp.sum(kept, axis=1, keepdims=True), (8, 128))
    marks = marks.astype(jnp.bfloat16)
    for d in range(16):
        out[d, MARK_ROW // 8] = marks
    for i in range(3):
        for copy in copies[4 * i : 4 * i + 4]:
            copy.wait()
        count, step = (TILES, 8) if i == 2 else (HALO, 7)
        base = (0, 2 * HALO, Q_ROW // 8)[i]
        for h in range(HEADS):
            for half in range(2):
                for r in range(2):
                    for w in range(count):
                        out[2 * h + half, base + 2 * w + r] = buf[
                            i, r, step * half + w, :, pl.ds(h * D, D)
                        ]


def pack(q, k, v, window):
    shaped = [
        pltpu.with_memory_space_constraint(x.reshape(2, COLS, 8, HEADS * D), pltpu.HBM)
        for x in (q, k, v)
    ]
    anywhere = pl.BlockSpec(memory_space=pl.ANY)
    return pl.pallas_call(
        pack_kernel,
        out_shape=pltpu.VMEM((16, ROWS // 8, 8, D), jnp.bfloat16),
        in_specs=[anywhere] * 4,
        out_specs=VMEM,
        scratch_shapes=[
            pltpu.VMEM((3, 2, COLS, 8, HEADS * D), jnp.bfloat16),
            pltpu.VMEM((1, 27), jnp.int32),
            pltpu.SemaphoreType.DMA((3, 2, 2)),
            pltpu.SemaphoreType.DMA,
        ],
        compiler_params=limit(16),
        name="pack",
    )(*shaped, pltpu.with_memory_space_constraint(window.reshape(1, 27), pltpu.HBM))


def cut_kernel(all_ref, first_ref, last_ref):
    for part in range(2):
        row = HALO * 16 * part
        first_ref[:, FIRST * part : FIRST * (part + 1)] = all_ref[:, row : row + FIRST]
        last_ref[:, LAST * part : LAST * (part + 1)] = all_ref[:, row + FIRST : row + HALO * 16]


def cut(everything):
    return pl.pallas_call(
        cut_kernel,
        out_shape=(
            pltpu.VMEM((16, 2 * FIRST, D), jnp.bfloat16),
            pltpu.VMEM((16, 2 * LAST, D), jnp.bfloat16),
        ),
        in_specs=[VMEM],
        out_specs=(VMEM, VMEM),
        compiler_params=limit(8),
        name="cut",
    )(resident(everything))


def take(ref, row):
    start = pl.multiple_of(row, 16)
    return ref[:, pl.ds(start, 16), :].reshape(256, D)


def shard_place():
    t = lax.axis_index("temporal")
    half = lax.axis_index("spatial") % 2
    return t, half


def key_index(w, b, half):
    return jnp.clip(w + b - 1 + half, 0, HALO - 1)


def columns_ok(column, b):
    return (column + b - 1 >= 0) & (column + b - 1 < COLS)


def scores(q, k):
    return lax.dot_general(q, k, (((1,), (1,)), ((), ())), preferred_element_type=jnp.float32)


def weigh(s_ref, slot, refs, oks, shift_from, total, acc):
    for n, value in enumerate(refs):
        v = value()
        shift = shift_from if oks[n] is None else jnp.where(oks[n], shift_from, BIG)
        p = jnp.exp2(s_ref[slot, :, n * 256 : (n + 1) * 256] * SCALE - shift)
        part = p[:, 0:128] + p[:, 128:256]
        total = part if total is None else total + part
        mixed = jnp.dot(p.astype(jnp.bfloat16), v, preferred_element_type=jnp.float32)
        acc = mixed if acc is None else acc + mixed
    return total, acc


def near_kernel(all_ref, mate_ref, acc_ref, peak_ref, total_ref, s_ref):
    t, half = shard_place()
    even = t % 2 == 0

    def tile(w, slot):
        column = half * TILES + w
        q = take(all_ref, Q_ROW + 16 * w)
        marks = all_ref[column, pl.ds(MARK_ROW, 8), :].astype(jnp.float32)
        refs, oks, top = [], [], None
        for ref in (all_ref, mate_ref):
            for b in range(3):
                n = len(refs)
                row = key_index(w, b, half) * 16
                k = take(ref, row)
                s = scores(q, k)
                s_ref[slot, :, n * 256 : (n + 1) * 256] = s
                high = jnp.max(s, axis=1, keepdims=True)
                if ref is all_ref:
                    mark = None if b == 1 else marks[3 + b // 2 : 4 + b // 2, 0:1]
                else:
                    mark = jnp.where(even, marks[5 + b : 6 + b, 0:1], marks[b : b + 1, 0:1])
                if mark is None:
                    ok = None
                else:
                    gate = 1.0 if b == 1 else jnp.where(columns_ok(column, b), 1.0, 0.0)
                    ok = jnp.broadcast_to(mark * gate, (256, 1)) > 0.5
                    high = jnp.where(ok, high, -BIG)
                top = high if top is None else jnp.maximum(top, high)
                refs.append(functools.partial(take, ref, row + HALO * 16))
                oks.append(ok)
        peak = top * SCALE
        total, acc = weigh(s_ref, slot, refs, oks, peak, None, None)
        acc_ref[w] = acc
        total_ref[w] = total
        peak_ref[w] = jnp.broadcast_to(peak, (256, 128))

    def pair(i, carry):
        tile(2 * i, 0)
        tile(2 * i + 1, 1)
        return carry

    lax.fori_loop(0, TILES // 2, pair, 0)


def near(everything, mate):
    part = pltpu.VMEM((TILES, 256, D), jnp.float32)
    return pl.pallas_call(
        near_kernel,
        out_shape=(part, part, part),
        in_specs=[VMEM] * 2,
        out_specs=(VMEM,) * 3,
        scratch_shapes=[pltpu.VMEM((2, 256, 6 * 256), jnp.float32)],
        compiler_params=limit(16),
        cost_estimate=pl.CostEstimate(
            flops=8 * 6 * 4 * 256 * 256 * D, bytes_accessed=6 << 20, transcendentals=8 * 6 * 65536
        ),
        name="near",
    )(resident(everything), resident(mate))


def far_take(first_ref, last_ref, w, b, half, part):
    spot = w + b - 1
    index = key_index(w, b, half)
    early = functools.partial(take, first_ref)
    if spot < 6:
        return early(FIRST * part + index * 16)
    late = functools.partial(take, last_ref)
    if spot > 6:
        return late(LAST * part + (index - 7) * 16)
    return jnp.where(half == 0, early(FIRST * part + 6 * 16), late(LAST * part))


def far_kernel(tiles, all_ref, first_ref, last_ref, acc_ref, peak_ref, total_ref, o_ref, s_ref):
    t, half = shard_place()
    even = t % 2 == 0
    t_ok = jnp.where(even, t > 0, t < 7)
    for slot, w in enumerate(tiles):
        column = half * TILES + w
        q = take(all_ref, Q_ROW + 16 * w)
        marks = all_ref[column, pl.ds(MARK_ROW, 8), :].astype(jnp.float32)
        refs, oks = [], []
        before = peak_ref[w, :, 0:1]
        top = None
        for b in range(3):
            s = scores(q, far_take(first_ref, last_ref, w, b, half, 0))
            s_ref[slot, :, b * 256 : (b + 1) * 256] = s
            mark = jnp.where(even, marks[b : b + 1, 0:1], marks[5 + b : 6 + b, 0:1])
            gate = jnp.where(columns_ok(column, b) & t_ok, 1.0, 0.0)
            ok = jnp.broadcast_to(mark * gate, (256, 1)) > 0.5
            high = jnp.where(ok, jnp.max(s, axis=1, keepdims=True), -BIG)
            top = high if top is None else jnp.maximum(top, high)
            refs.append(functools.partial(far_take, first_ref, last_ref, w, b, half, 1))
            oks.append(ok)
        peak = jnp.maximum(before, jnp.where(top > -BIG, top, -BIG / 4) * SCALE)
        fade = jnp.exp2(before - peak)
        total, acc = weigh(
            s_ref, slot, refs, oks, peak, total_ref[w] * fade, acc_ref[w] * fade
        )
        out = acc / jnp.sum(total, axis=1, keepdims=True)
        o_ref[:, 16 * w : 16 * w + 16, :] = out.astype(jnp.bfloat16).reshape(16, 16, D)


def far_early_kernel(all_ref, first_ref, acc_ref, peak_ref, total_ref, o_ref, s_ref):
    far_kernel(
        range(EARLY), all_ref, first_ref, None, acc_ref, peak_ref, total_ref, o_ref, s_ref
    )


def far_late_kernel(all_ref, first_ref, last_ref, acc_ref, peak_ref, total_ref, _, o_ref, s_ref):
    far_kernel(
        range(EARLY, TILES), all_ref, first_ref, last_ref, acc_ref, peak_ref, total_ref, o_ref, s_ref
    )


def far(kernel, name, count, operands, aliases):
    return pl.pallas_call(
        kernel,
        out_shape=pltpu.VMEM((16, TILES * 16, D), jnp.bfloat16),
        in_specs=[VMEM] * len(operands),
        out_specs=VMEM,
        scratch_shapes=[pltpu.VMEM((count, 256, 3 * 256), jnp.float32)],
        compiler_params=limit(16),
        input_output_aliases=aliases,
        cost_estimate=pl.CostEstimate(
            flops=count * 3 * 4 * 256 * 256 * D,
            bytes_accessed=count << 19,
            transcendentals=count * 3 * 65536,
        ),
        name=name,
    )(*[resident(x) for x in operands])


def unpack_kernel(x_ref, o_ref):
    for h in range(HEADS):
        for half in range(2):
            for r in range(2):
                o_ref[r, pl.ds(8 * half, TILES), :, pl.ds(h * D, D)] = x_ref[2 * h + half, :, r]


def unpack(x):
    out = pl.pallas_call(
        unpack_kernel,
        out_shape=jax.ShapeDtypeStruct((2, COLS, 8, HEADS * D), jnp.bfloat16),
        in_specs=[VMEM],
        out_specs=VMEM,
        compiler_params=limit(8),
        name="unpack",
    )(resident(x))
    return out.reshape(256, HEADS * D)


def swap(x):
    return lax.all_to_all(x, "spatial", split_axis=0, concat_axis=0, tiled=True)


def body(queries, keys, values, window):
    everything = swap(pack(queries, keys, values, window).reshape(16, ROWS, D))
    first, last = cut(everything)
    steps = lax.axis_size("temporal")
    across = [(i, i + 1) for i in range(1, steps - 1, 2)]
    across = across + [(j, i) for i, j in across]
    mates = [(i, i + 1) for i in range(0, steps, 2)]
    mates = mates + [(j, i) for i, j in mates]
    far_first = lax.ppermute(first, "temporal", across)
    far_last = lax.ppermute(last, "temporal", across)
    mate = lax.ppermute(everything, "temporal", mates)
    parts = near(everything, mate)
    out = far(far_early_kernel, "far_early", EARLY, (everything, far_first, *parts), {})
    out = far(
        far_late_kernel,
        "far_late",
        TILES - EARLY,
        (everything, far_first, far_last, *parts, out),
        {6: 0},
    )
    back = swap(out)
    return unpack(back.reshape(16, TILES, 2, 8, D))


def solution(mesh):
    return jax.shard_map(
        body,
        mesh=mesh,
        in_specs=(
            P(("temporal", "spatial"), "head"),
            P(("temporal", "spatial"), "head"),
            P(("temporal", "spatial"), "head"),
            P("temporal", None, "spatial", None),
        ),
        out_specs=P(("temporal", "spatial"), "head"),
        check_vma=False,
    )
```

```python
import functools
import math

import jax
import jax.numpy as jnp
from jax import lax
from jax.experimental import pallas as pl
from jax.experimental.pallas import tpu as pltpu
from jax.sharding import PartitionSpec as P

D = 128
HEADS = 8
TILES = 8
COLS = 16
HALO = 9
KV_ROWS = 2 * HALO * 16
Q_ROW = KV_ROWS
MARK_ROW = KV_ROWS + TILES * 16
ROWS = MARK_ROW + 8
FIRST = 7 * 16
LAST = 2 * 16
EARLY = 5
BIG = 3.0e38
SCALE = math.log2(math.e) / math.sqrt(D)
VMEM = pl.BlockSpec(memory_space=pltpu.VMEM)


def resident(x):
    return pltpu.with_memory_space_constraint(x, pltpu.VMEM)


def limit(mib):
    return pltpu.CompilerParams(vmem_limit_bytes=mib << 20)


def pack_kernel(q_hbm, k_hbm, v_hbm, w_hbm, out, buf, w_ref, sems, w_sem):
    fetch = pltpu.make_async_copy(w_hbm, w_ref, w_sem)
    fetch.start()
    copies = []
    for i, src in enumerate((k_hbm, v_hbm, q_hbm)):
        for r in range(2):
            for part in range(2):
                cut = pl.ds(8 * part, 8)
                copies.append(
                    pltpu.make_async_copy(
                        src.at[r, cut], buf.at[i, r, cut], sems.at[i, r, part]
                    )
                )
    for copy in copies:
        copy.start()
    fetch.wait()
    pattern = w_ref[...].astype(jnp.float32)
    pattern = jnp.concatenate([pattern, jnp.zeros((1, 101), jnp.float32)], axis=1)
    row = lax.broadcasted_iota(jnp.int32, (8, 128), 0)
    lanes = lax.broadcasted_iota(jnp.int32, (8, 128), 1)
    entry = row + jnp.where(row >= 4, 1, 0)
    pick = 9 * (entry // 3) + 3 + entry % 3
    kept = jnp.where(lanes == pick, jnp.broadcast_to(pattern, (8, 128)), 0.0)
    marks = jnp.broadcast_to(jnp.sum(kept, axis=1, keepdims=True), (8, 128))
    marks = marks.astype(jnp.bfloat16)
    for d in range(16):
        out[d, MARK_ROW // 8] = marks
    for i in range(3):
        for copy in copies[4 * i : 4 * i + 4]:
            copy.wait()
        count, step = (TILES, 8) if i == 2 else (HALO, 7)
        base = (0, 2 * HALO, Q_ROW // 8)[i]
        for h in range(HEADS):
            for half in range(2):
                for r in range(2):
                    for w in range(count):
                        out[2 * h + half, base + 2 * w + r] = buf[
                            i, r, step * half + w, :, pl.ds(h * D, D)
                        ]


def pack(q, k, v, window):
    shaped = [
        pltpu.with_memory_space_constraint(x.reshape(2, COLS, 8, HEADS * D), pltpu.HBM)
        for x in (q, k, v)
    ]
    anywhere = pl.BlockSpec(memory_space=pl.ANY)
    return pl.pallas_call(
        pack_kernel,
        out_shape=pltpu.VMEM((16, ROWS // 8, 8, D), jnp.bfloat16),
        in_specs=[anywhere] * 4,
        out_specs=VMEM,
        scratch_shapes=[
            pltpu.VMEM((3, 2, COLS, 8, HEADS * D), jnp.bfloat16),
            pltpu.VMEM((1, 27), jnp.int32),
            pltpu.SemaphoreType.DMA((3, 2, 2)),
            pltpu.SemaphoreType.DMA,
        ],
        compiler_params=limit(16),
        name="pack",
    )(*shaped, pltpu.with_memory_space_constraint(window.reshape(1, 27), pltpu.HBM))


def cut_kernel(all_ref, first_ref, last_ref):
    for part in range(2):
        row = HALO * 16 * part
        first_ref[:, FIRST * part : FIRST * (part + 1)] = all_ref[:, row : row + FIRST]
        last_ref[:, LAST * part : LAST * (part + 1)] = all_ref[:, row + FIRST : row + HALO * 16]


def cut(everything):
    return pl.pallas_call(
        cut_kernel,
        out_shape=(
            pltpu.VMEM((16, 2 * FIRST, D), jnp.bfloat16),
            pltpu.VMEM((16, 2 * LAST, D), jnp.bfloat16),
        ),
        in_specs=[VMEM],
        out_specs=(VMEM, VMEM),
        compiler_params=limit(8),
        name="cut",
    )(resident(everything))


def take(ref, row):
    start = pl.multiple_of(row, 16)
    return ref[:, pl.ds(start, 16), :].reshape(256, D)


def shard_place():
    t = lax.axis_index("temporal")
    half = lax.axis_index("spatial") % 2
    return t, half


def key_index(w, b, half):
    return jnp.clip(w + b - 1 + half, 0, HALO - 1)


def columns_ok(column, b):
    return (column + b - 1 >= 0) & (column + b - 1 < COLS)


def scores(q, k):
    return lax.dot_general(q, k, (((1,), (1,)), ((), ())), preferred_element_type=jnp.float32)


def weigh(s_ref, slot, refs, oks, shift_from, total, acc):
    for n, value in enumerate(refs):
        v = value()
        shift = shift_from if oks[n] is None else jnp.where(oks[n], shift_from, BIG)
        p = jnp.exp2(s_ref[slot, :, n * 256 : (n + 1) * 256] * SCALE - shift)
        part = p[:, 0:128] + p[:, 128:256]
        total = part if total is None else total + part
        mixed = jnp.dot(p.astype(jnp.bfloat16), v, preferred_element_type=jnp.float32)
        acc = mixed if acc is None else acc + mixed
    return total, acc


def near_kernel(all_ref, mate_ref, acc_ref, peak_ref, total_ref, s_ref):
    t, half = shard_place()
    even = t % 2 == 0

    def tile(w, slot):
        column = half * TILES + w
        q = take(all_ref, Q_ROW + 16 * w)
        marks = all_ref[column, pl.ds(MARK_ROW, 8), :].astype(jnp.float32)
        refs, oks, top = [], [], None
        for ref in (all_ref, mate_ref):
            for b in range(3):
                n = len(refs)
                row = key_index(w, b, half) * 16
                k = take(ref, row)
                s = scores(q, k)
                s_ref[slot, :, n * 256 : (n + 1) * 256] = s
                high = jnp.max(s, axis=1, keepdims=True)
                if ref is all_ref:
                    mark = None if b == 1 else marks[3 + b // 2 : 4 + b // 2, 0:1]
                else:
                    mark = jnp.where(even, marks[5 + b : 6 + b, 0:1], marks[b : b + 1, 0:1])
                if mark is None:
                    ok = None
                else:
                    gate = 1.0 if b == 1 else jnp.where(columns_ok(column, b), 1.0, 0.0)
                    ok = jnp.broadcast_to(mark * gate, (256, 1)) > 0.5
                    high = jnp.where(ok, high, -BIG)
                top = high if top is None else jnp.maximum(top, high)
                refs.append(functools.partial(take, ref, row + HALO * 16))
                oks.append(ok)
        peak = top * SCALE
        total, acc = weigh(s_ref, slot, refs, oks, peak, None, None)
        acc_ref[w] = acc
        total_ref[w] = total
        peak_ref[w] = jnp.broadcast_to(peak, (256, 128))

    def pair(i, carry):
        tile(2 * i, 0)
        tile(2 * i + 1, 1)
        return carry

    lax.fori_loop(0, TILES // 2, pair, 0)


def near(everything, mate):
    part = pltpu.VMEM((TILES, 256, D), jnp.float32)
    return pl.pallas_call(
        near_kernel,
        out_shape=(part, part, part),
        in_specs=[VMEM] * 2,
        out_specs=(VMEM,) * 3,
        scratch_shapes=[pltpu.VMEM((2, 256, 6 * 256), jnp.float32)],
        compiler_params=limit(16),
        cost_estimate=pl.CostEstimate(
            flops=8 * 6 * 4 * 256 * 256 * D, bytes_accessed=6 << 20, transcendentals=8 * 6 * 65536
        ),
        name="near",
    )(resident(everything), resident(mate))


def far_take(first_ref, last_ref, w, b, half, part):
    spot = w + b - 1
    index = key_index(w, b, half)
    early = functools.partial(take, first_ref)
    if spot < 6:
        return early(FIRST * part + index * 16)
    late = functools.partial(take, last_ref)
    if spot > 6:
        return late(LAST * part + (index - 7) * 16)
    return jnp.where(half == 0, early(FIRST * part + 6 * 16), late(LAST * part))


def far_kernel(tiles, all_ref, first_ref, last_ref, acc_ref, peak_ref, total_ref, o_ref, s_ref):
    t, half = shard_place()
    even = t % 2 == 0
    t_ok = jnp.where(even, t > 0, t < 7)
    for slot, w in enumerate(tiles):
        column = half * TILES + w
        q = take(all_ref, Q_ROW + 16 * w)
        marks = all_ref[column, pl.ds(MARK_ROW, 8), :].astype(jnp.float32)
        refs, oks = [], []
        before = peak_ref[w, :, 0:1]
        top = None
        for b in range(3):
            s = scores(q, far_take(first_ref, last_ref, w, b, half, 0))
            s_ref[slot, :, b * 256 : (b + 1) * 256] = s
            mark = jnp.where(even, marks[b : b + 1, 0:1], marks[5 + b : 6 + b, 0:1])
            gate = jnp.where(columns_ok(column, b) & t_ok, 1.0, 0.0)
            ok = jnp.broadcast_to(mark * gate, (256, 1)) > 0.5
            high = jnp.where(ok, jnp.max(s, axis=1, keepdims=True), -BIG)
            top = high if top is None else jnp.maximum(top, high)
            refs.append(functools.partial(far_take, first_ref, last_ref, w, b, half, 1))
            oks.append(ok)
        peak = jnp.maximum(before, jnp.where(top > -BIG, top, -BIG / 4) * SCALE)
        fade = jnp.exp2(before - peak)
        total, acc = weigh(
            s_ref, slot, refs, oks, peak, total_ref[w] * fade, acc_ref[w] * fade
        )
        out = acc / jnp.sum(total, axis=1, keepdims=True)
        o_ref[:, 16 * w : 16 * w + 16, :] = out.astype(jnp.bfloat16).reshape(16, 16, D)


def far_early_kernel(all_ref, first_ref, acc_ref, peak_ref, total_ref, o_ref, s_ref):
    far_kernel(
        range(EARLY), all_ref, first_ref, None, acc_ref, peak_ref, total_ref, o_ref, s_ref
    )


def far_late_kernel(all_ref, first_ref, last_ref, acc_ref, peak_ref, total_ref, _, o_ref, s_ref):
    far_kernel(
        range(EARLY, TILES), all_ref, first_ref, last_ref, acc_ref, peak_ref, total_ref, o_ref, s_ref
    )


def far(kernel, count, operands, aliases):
    return pl.pallas_call(
        kernel,
        out_shape=pltpu.VMEM((16, TILES * 16, D), jnp.bfloat16),
        in_specs=[VMEM] * len(operands),
        out_specs=VMEM,
        scratch_shapes=[pltpu.VMEM((count, 256, 3 * 256), jnp.float32)],
        compiler_params=limit(16),
        input_output_aliases=aliases,
        cost_estimate=pl.CostEstimate(
            flops=count * 3 * 4 * 256 * 256 * D,
            bytes_accessed=count << 19,
            transcendentals=count * 3 * 65536,
        ),
    )(*[resident(x) for x in operands])


def unpack_kernel(x_ref, o_hbm, buf, sems):
    copies = []
    for r in range(2):
        for half in range(2):
            cut_out = pl.ds(8 * half, TILES)
            for h in range(HEADS):
                buf[r, cut_out, :, pl.ds(h * D, D)] = x_ref[2 * h + half, :, r]
            copy = pltpu.make_async_copy(
                buf.at[r, cut_out], o_hbm.at[r, cut_out], sems.at[r, half]
            )
            copy.start()
            copies.append(copy)
    for copy in copies:
        copy.wait()


def unpack(x):
    shape = (2, COLS, 8, HEADS * D)
    out = pl.pallas_call(
        unpack_kernel,
        out_shape=jax.ShapeDtypeStruct(shape, jnp.bfloat16),
        in_specs=[VMEM],
        out_specs=pl.BlockSpec(memory_space=pl.ANY),
        scratch_shapes=[pltpu.VMEM(shape, jnp.bfloat16), pltpu.SemaphoreType.DMA((2, 2))],
        compiler_params=limit(8),
        name="unpack",
    )(resident(x))
    return out.reshape(256, HEADS * D)


def swap(x):
    return lax.all_to_all(x, "spatial", split_axis=0, concat_axis=0, tiled=True)


def body(queries, keys, values, window):
    everything = swap(pack(queries, keys, values, window).reshape(16, ROWS, D))
    first, last = cut(everything)
    steps = lax.axis_size("temporal")
    across = [(i, i + 1) for i in range(1, steps - 1, 2)]
    across = across + [(j, i) for i, j in across]
    mates = [(i, i + 1) for i in range(0, steps, 2)]
    mates = mates + [(j, i) for i, j in mates]
    far_first = lax.ppermute(first, "temporal", across)
    mate = lax.ppermute(everything, "temporal", mates)
    far_last = lax.ppermute(last, "temporal", across)
    parts = near(everything, mate)
    out = far(far_early_kernel, EARLY, (everything, far_first, *parts), {})
    out = far(
        far_late_kernel, TILES - EARLY, (everything, far_first, far_last, *parts, out), {6: 0}
    )
    back = swap(out)
    return unpack(back.reshape(16, TILES, 2, 8, D))


def solution(mesh):
    return jax.shard_map(
        body,
        mesh=mesh,
        in_specs=(
            P(("temporal", "spatial"), "head"),
            P(("temporal", "spatial"), "head"),
            P(("temporal", "spatial"), "head"),
            P("temporal", None, "spatial", None),
        ),
        out_specs=P(("temporal", "spatial"), "head"),
        check_vma=False,
    )
```

```python
import functools
import math

import jax
import jax.numpy as jnp
from jax import lax
from jax.experimental import pallas as pl
from jax.experimental.pallas import tpu as pltpu
from jax.sharding import PartitionSpec as P

D = 128
HEADS = 8
TILES = 8
COLS = 16
HALO = 9
KV_ROWS = 2 * HALO * 16
Q_ROW = KV_ROWS
MARK_ROW = KV_ROWS + TILES * 16
ROWS = MARK_ROW + 8
FIRST = 7 * 16
LAST = 2 * 16
EARLY = 5
BIG = 3.0e38
SCALE = math.log2(math.e) / math.sqrt(D)
VMEM = pl.BlockSpec(memory_space=pltpu.VMEM)


def resident(x):
    return pltpu.with_memory_space_constraint(x, pltpu.VMEM)


def limit(mib):
    return pltpu.CompilerParams(vmem_limit_bytes=mib << 20)


def pack_kernel(q_hbm, k_hbm, v_hbm, w_hbm, out, buf, w_ref, sems, w_sem):
    fetch = pltpu.make_async_copy(w_hbm, w_ref, w_sem)
    fetch.start()
    copies = []
    for i, src in enumerate((k_hbm, v_hbm, q_hbm)):
        for r in range(2):
            for part in range(2):
                cut = pl.ds(8 * part, 8)
                copies.append(
                    pltpu.make_async_copy(
                        src.at[r, cut], buf.at[i, r, cut], sems.at[i, r, part]
                    )
                )
    for copy in copies:
        copy.start()
    fetch.wait()
    pattern = w_ref[...].astype(jnp.float32)
    pattern = jnp.concatenate([pattern, jnp.zeros((1, 101), jnp.float32)], axis=1)
    row = lax.broadcasted_iota(jnp.int32, (8, 128), 0)
    lanes = lax.broadcasted_iota(jnp.int32, (8, 128), 1)
    entry = row + jnp.where(row >= 4, 1, 0)
    pick = 9 * (entry // 3) + 3 + entry % 3
    kept = jnp.where(lanes == pick, jnp.broadcast_to(pattern, (8, 128)), 0.0)
    marks = jnp.broadcast_to(jnp.sum(kept, axis=1, keepdims=True), (8, 128))
    marks = marks.astype(jnp.bfloat16)
    for d in range(16):
        out[d, MARK_ROW // 8] = marks
    for i in range(3):
        for copy in copies[4 * i : 4 * i + 4]:
            copy.wait()
        count, step = (TILES, 8) if i == 2 else (HALO, 7)
        base = (0, 2 * HALO, Q_ROW // 8)[i]
        for h in range(HEADS):
            for half in range(2):
                for r in range(2):
                    for w in range(count):
                        out[2 * h + half, base + 2 * w + r] = buf[
                            i, r, step * half + w, :, pl.ds(h * D, D)
                        ]


def pack(q, k, v, window):
    shaped = [
        pltpu.with_memory_space_constraint(x.reshape(2, COLS, 8, HEADS * D), pltpu.HBM)
        for x in (q, k, v)
    ]
    anywhere = pl.BlockSpec(memory_space=pl.ANY)
    return pl.pallas_call(
        pack_kernel,
        out_shape=pltpu.VMEM((16, ROWS // 8, 8, D), jnp.bfloat16),
        in_specs=[anywhere] * 4,
        out_specs=VMEM,
        scratch_shapes=[
            pltpu.VMEM((3, 2, COLS, 8, HEADS * D), jnp.bfloat16),
            pltpu.VMEM((1, 27), jnp.int32),
            pltpu.SemaphoreType.DMA((3, 2, 2)),
            pltpu.SemaphoreType.DMA,
        ],
        compiler_params=limit(16),
        name="pack",
    )(*shaped, pltpu.with_memory_space_constraint(window.reshape(1, 27), pltpu.HBM))


def cut_kernel(all_ref, first_ref, last_ref, both_ref):
    both_ref[...] = all_ref[:, 0:KV_ROWS]
    for part in range(2):
        row = HALO * 16 * part
        first_ref[:, FIRST * part : FIRST * (part + 1)] = all_ref[:, row : row + FIRST]
        last_ref[:, LAST * part : LAST * (part + 1)] = all_ref[:, row + FIRST : row + HALO * 16]


def cut(everything):
    return pl.pallas_call(
        cut_kernel,
        out_shape=(
            pltpu.VMEM((16, 2 * FIRST, D), jnp.bfloat16),
            pltpu.VMEM((16, 2 * LAST, D), jnp.bfloat16),
            pltpu.VMEM((16, KV_ROWS, D), jnp.bfloat16),
        ),
        in_specs=[VMEM],
        out_specs=(VMEM,) * 3,
        compiler_params=limit(8),
        name="cut",
    )(resident(everything))


def take(ref, row):
    start = pl.multiple_of(row, 16)
    return ref[:, pl.ds(start, 16), :].reshape(256, D)


def shard_place():
    t = lax.axis_index("temporal")
    half = lax.axis_index("spatial") % 2
    return t, half


def key_index(w, b, half):
    return jnp.clip(w + b - 1 + half, 0, HALO - 1)


def columns_ok(column, b):
    return (column + b - 1 >= 0) & (column + b - 1 < COLS)


def scores(q, k):
    return lax.dot_general(q, k, (((1,), (1,)), ((), ())), preferred_element_type=jnp.float32)


def weigh(s_ref, slot, refs, oks, shift_from, total, acc):
    for n, value in enumerate(refs):
        v = value()
        shift = shift_from if oks[n] is None else jnp.where(oks[n], shift_from, BIG)
        p = jnp.exp2(s_ref[slot, :, n * 256 : (n + 1) * 256] * SCALE - shift)
        part = p[:, 0:128] + p[:, 128:256]
        total = part if total is None else total + part
        mixed = jnp.dot(p.astype(jnp.bfloat16), v, preferred_element_type=jnp.float32)
        acc = mixed if acc is None else acc + mixed
    return total, acc


def near_kernel(all_ref, mate_ref, acc_ref, peak_ref, total_ref, s_ref):
    t, half = shard_place()
    even = t % 2 == 0

    def tile(w, slot):
        column = half * TILES + w
        q = take(all_ref, Q_ROW + 16 * w)
        marks = all_ref[column, pl.ds(MARK_ROW, 8), :].astype(jnp.float32)
        refs, oks, top = [], [], None
        for ref in (all_ref, mate_ref):
            for b in range(3):
                n = len(refs)
                row = key_index(w, b, half) * 16
                k = take(ref, row)
                s = scores(q, k)
                s_ref[slot, :, n * 256 : (n + 1) * 256] = s
                high = jnp.max(s, axis=1, keepdims=True)
                if ref is all_ref:
                    mark = None if b == 1 else marks[3 + b // 2 : 4 + b // 2, 0:1]
                else:
                    mark = jnp.where(even, marks[5 + b : 6 + b, 0:1], marks[b : b + 1, 0:1])
                if mark is None:
                    ok = None
                else:
                    gate = 1.0 if b == 1 else jnp.where(columns_ok(column, b), 1.0, 0.0)
                    ok = jnp.broadcast_to(mark * gate, (256, 1)) > 0.5
                    high = jnp.where(ok, high, -BIG)
                top = high if top is None else jnp.maximum(top, high)
                refs.append(functools.partial(take, ref, row + HALO * 16))
                oks.append(ok)
        peak = top * SCALE
        total, acc = weigh(s_ref, slot, refs, oks, peak, None, None)
        acc_ref[w] = acc
        total_ref[w] = total
        peak_ref[w] = jnp.broadcast_to(peak, (256, 128))

    def pair(i, carry):
        tile(2 * i, 0)
        tile(2 * i + 1, 1)
        return carry

    lax.fori_loop(0, TILES // 2, pair, 0)


def near(everything, mate):
    part = pltpu.VMEM((TILES, 256, D), jnp.float32)
    return pl.pallas_call(
        near_kernel,
        out_shape=(part, part, part),
        in_specs=[VMEM] * 2,
        out_specs=(VMEM,) * 3,
        scratch_shapes=[pltpu.VMEM((2, 256, 6 * 256), jnp.float32)],
        compiler_params=limit(16),
        cost_estimate=pl.CostEstimate(
            flops=8 * 6 * 4 * 256 * 256 * D, bytes_accessed=6 << 20, transcendentals=8 * 6 * 65536
        ),
        name="near",
    )(resident(everything), resident(mate))


def far_take(first_ref, last_ref, w, b, half, part):
    spot = w + b - 1
    index = key_index(w, b, half)
    early = functools.partial(take, first_ref)
    if spot < 6:
        return early(FIRST * part + index * 16)
    late = functools.partial(take, last_ref)
    if spot > 6:
        return late(LAST * part + (index - 7) * 16)
    return jnp.where(half == 0, early(FIRST * part + 6 * 16), late(LAST * part))


def far_kernel(tiles, all_ref, first_ref, last_ref, acc_ref, peak_ref, total_ref, o_ref, s_ref):
    t, half = shard_place()
    even = t % 2 == 0
    t_ok = jnp.where(even, t > 0, t < 7)
    for slot, w in enumerate(tiles):
        column = half * TILES + w
        q = take(all_ref, Q_ROW + 16 * w)
        marks = all_ref[column, pl.ds(MARK_ROW, 8), :].astype(jnp.float32)
        refs, oks = [], []
        before = peak_ref[w, :, 0:1]
        top = None
        for b in range(3):
            s = scores(q, far_take(first_ref, last_ref, w, b, half, 0))
            s_ref[slot, :, b * 256 : (b + 1) * 256] = s
            mark = jnp.where(even, marks[b : b + 1, 0:1], marks[5 + b : 6 + b, 0:1])
            gate = jnp.where(columns_ok(column, b) & t_ok, 1.0, 0.0)
            ok = jnp.broadcast_to(mark * gate, (256, 1)) > 0.5
            high = jnp.where(ok, jnp.max(s, axis=1, keepdims=True), -BIG)
            top = high if top is None else jnp.maximum(top, high)
            refs.append(functools.partial(far_take, first_ref, last_ref, w, b, half, 1))
            oks.append(ok)
        peak = jnp.maximum(before, jnp.where(top > -BIG, top, -BIG / 4) * SCALE)
        fade = jnp.exp2(before - peak)
        total, acc = weigh(
            s_ref, slot, refs, oks, peak, total_ref[w] * fade, acc_ref[w] * fade
        )
        out = acc / jnp.sum(total, axis=1, keepdims=True)
        o_ref[:, 16 * w : 16 * w + 16, :] = out.astype(jnp.bfloat16).reshape(16, 16, D)


def far_early_kernel(all_ref, first_ref, acc_ref, peak_ref, total_ref, o_ref, s_ref):
    far_kernel(
        range(EARLY), all_ref, first_ref, None, acc_ref, peak_ref, total_ref, o_ref, s_ref
    )


def far_late_kernel(all_ref, first_ref, last_ref, acc_ref, peak_ref, total_ref, _, o_ref, s_ref):
    far_kernel(
        range(EARLY, TILES), all_ref, first_ref, last_ref, acc_ref, peak_ref, total_ref, o_ref, s_ref
    )


def far(kernel, count, operands, aliases):
    return pl.pallas_call(
        kernel,
        out_shape=pltpu.VMEM((16, TILES * 16, D), jnp.bfloat16),
        in_specs=[VMEM] * len(operands),
        out_specs=VMEM,
        scratch_shapes=[pltpu.VMEM((count, 256, 3 * 256), jnp.float32)],
        compiler_params=limit(16),
        input_output_aliases=aliases,
        cost_estimate=pl.CostEstimate(
            flops=count * 3 * 4 * 256 * 256 * D,
            bytes_accessed=count << 19,
            transcendentals=count * 3 * 65536,
        ),
    )(*[resident(x) for x in operands])


def unpack_kernel(x_ref, o_hbm, buf, sems):
    copies = []
    for r in range(2):
        for half in range(2):
            cut_out = pl.ds(8 * half, TILES)
            for h in range(HEADS):
                buf[r, cut_out, :, pl.ds(h * D, D)] = x_ref[2 * h + half, :, r]
            copy = pltpu.make_async_copy(
                buf.at[r, cut_out], o_hbm.at[r, cut_out], sems.at[r, half]
            )
            copy.start()
            copies.append(copy)
    for copy in copies:
        copy.wait()


def unpack(x):
    shape = (2, COLS, 8, HEADS * D)
    out = pl.pallas_call(
        unpack_kernel,
        out_shape=jax.ShapeDtypeStruct(shape, jnp.bfloat16),
        in_specs=[VMEM],
        out_specs=pl.BlockSpec(memory_space=pl.ANY),
        scratch_shapes=[pltpu.VMEM(shape, jnp.bfloat16), pltpu.SemaphoreType.DMA((2, 2))],
        compiler_params=limit(8),
        name="unpack",
    )(resident(x))
    return out.reshape(256, HEADS * D)


def swap(x):
    return lax.all_to_all(x, "spatial", split_axis=0, concat_axis=0, tiled=True)


def body(queries, keys, values, window):
    everything = swap(pack(queries, keys, values, window).reshape(16, ROWS, D))
    first, last, both = cut(everything)
    steps = lax.axis_size("temporal")
    across = [(i, i + 1) for i in range(1, steps - 1, 2)]
    across = across + [(j, i) for i, j in across]
    mates = [(i, i + 1) for i in range(0, steps, 2)]
    mates = mates + [(j, i) for i, j in mates]
    far_first = lax.ppermute(first, "temporal", across)
    mate = lax.ppermute(both, "temporal", mates)
    far_last = lax.ppermute(last, "temporal", across)
    parts = near(everything, mate)
    out = far(far_early_kernel, EARLY, (everything, far_first, *parts), {})
    out = far(
        far_late_kernel, TILES - EARLY, (everything, far_first, far_last, *parts, out), {6: 0}
    )
    back = swap(out)
    return unpack(back.reshape(16, TILES, 2, 8, D))


def solution(mesh):
    return jax.shard_map(
        body,
        mesh=mesh,
        in_specs=(
            P(("temporal", "spatial"), "head"),
            P(("temporal", "spatial"), "head"),
            P(("temporal", "spatial"), "head"),
            P("temporal", None, "spatial", None),
        ),
        out_specs=P(("temporal", "spatial"), "head"),
        check_vma=False,
    )
```
